32 devices in a mesh: seg: 4 (over y, core), sub: 8 (over z, x).
Axes of the slice: x: 2, y: 2, z: 4, core: 2. Of those that a mesh axis runs over, the one named last changes fastest.
Arguments:
- nodal_loads: float32 [4, 8, 32, 3072], P('seg', 'sub'), may hold values from -6 to 6
- schur_matrix: bfloat16 [4, 8, 3072, 3072], P('seg', 'sub'), may hold values from -2 to 9, as said below
- face_rows: int32 [4, 8, 3072], P('seg', 'sub'), may hold values from 0 to 3071, each once within a row
- face_len: int32 [4, 8, 2], replicated, may hold values from 192 to 768, as said below
- relax_step: float32 [4, 8], P('seg', 'sub'), may hold values from 0.03 to 0.1
- coarse_basis: float32 [4, 8, 4, 3072], P('seg', 'sub'), may hold values from -0.625 to 0.625
- primal_index: int32 [4, 8, 4], replicated, may hold values from 0 to 71, as said below
- coarse_inverse: float32 [72, 72], replicated, may hold values from -1 to 1.5, as said below
Outputs:
- solution: float32 [4, 8, 32, 3072], P('seg', 'sub')
- residual: float32 [4, 8, 32, 3072], P('seg', 'sub')
The draws below stay inside these ranges and needn't reach their ends.
Inputs may be any that keep to these rules, and one draw needn't show every extreme that they name: `schur_matrix`: symmetric in its last two dimensions and positive definite for each subdomain. `face_len`: entry [s, j, 0] counts the shared slots of the face between subdomains j and (j+1) mod 8 of segment s; entry [s, j, 1] those of the face between segments s and s+1 at subdomain j (not read for the last segment). Some entry [s, j, 0] equals 768. `primal_index`: one global number for each face: the face between subdomains j and (j+1) mod 8 of segment s, and the face below segment s at subdomain j (and above the last segment), numbered in a random order. Subdomains sharing a face name the same number; a face at the bridge's ends belongs to one subdomain only. `coarse_inverse`: symmetric positive definite.
All inputs are finite; a program needn't handle non-finite values.
Results may differ from the reference program's by a relative error of at most 0.0015.
Values sent between devices are 32-bit elements; how exact they have to be, the bound alone decides.
A program may use at most 128 MiB of HBM per device.

```python
import math
import jax
import jax.numpy as jnp
from jax import lax

NI = 3072
K = 32
DEG = 3
ITERS = 3
NF = 768
NP = 72
N_SEG = 4
N_SUB = 8


def draw_schur_matrix(key, part):

    def single(number):
        sub_key = jax.random.fold_in(jax.random.fold_in(key, 17), number)
        key_diag, key_noise = jax.random.split(sub_key)
        scales = jnp.exp(jax.random.uniform(key_diag, (NI,), jnp.float32, math.log(1.6), math.log(8.0)))
        noise = jax.random.normal(key_noise, (NI, NI), jnp.float32)
        sym_noise = (noise + noise.T) / math.sqrt(2.0 * NI)
        core = jnp.eye(NI, dtype=jnp.float32) + 0.3 * sym_noise
        roots = jnp.sqrt(scales)
        return (roots[:, None] * core * roots[None, :]).astype(jnp.bfloat16)
    stacked = lax.map(single, jnp.arange(N_SEG * N_SUB, dtype=jnp.int32))
    return stacked.reshape(N_SEG, N_SUB, NI, NI)


def draw_face_len(key, part):
    key_len, key_seg, key_sub = jax.random.split(jax.random.fold_in(key, 23), 3)
    values = jax.random.randint(key_len, (N_SEG, N_SUB, 2), NF // 4, NF + 1, jnp.int32)
    seg_pick = jax.random.randint(key_seg, (), 0, N_SEG, jnp.int32)
    sub_pick = jax.random.randint(key_sub, (), 0, N_SUB, jnp.int32)
    return values.at[seg_pick, sub_pick, 0].set(NF)


def draw_primal_index(key, part):
    order = jax.random.permutation(jax.random.fold_in(key, 29), NP).astype(jnp.int32)
    seg_ids = jnp.arange(N_SEG, dtype=jnp.int32)[:, None]
    sub_ids = jnp.arange(N_SUB, dtype=jnp.int32)[None, :]
    left_face = seg_ids * N_SUB + (sub_ids + N_SUB - 1) % N_SUB
    right_face = seg_ids * N_SUB + sub_ids
    down_face = N_SEG * N_SUB + seg_ids * N_SUB + sub_ids
    up_face = N_SEG * N_SUB + (seg_ids + 1) * N_SUB + sub_ids
    faces = jnp.stack([left_face, right_face, down_face, up_face], axis=2)
    return order[faces].astype(jnp.int32)


def draw_coarse_inverse(key, part):
    key_diag, key_noise = jax.random.split(jax.random.fold_in(key, 31))
    scales = jnp.exp(jax.random.uniform(key_diag, (NP,), jnp.float32, math.log(0.2), 0.0))
    noise = jax.random.normal(key_noise, (NP, NP), jnp.float32)
    sym_noise = (noise + noise.T) / math.sqrt(2.0 * NP)
    core = jnp.eye(NP, dtype=jnp.float32) + 0.3 * sym_noise
    roots = jnp.sqrt(scales)
    return roots[:, None] * core * roots[None, :]


def level_of(own_key, extent, cuts, smallest, largest):
    factor_of = 1.0
    for position, blocks in cuts:
        draws = jax.random.uniform(jax.random.fold_in(jax.random.fold_in(own_key, 6), position), (blocks,), jnp.float32, smallest / len(cuts), largest / len(cuts))
        factor_of = factor_of * jnp.repeat(jnp.exp(draws), extent[position] // blocks).reshape((-1,) + (1,) * (len(extent) - 1 - position))
    return factor_of


def centred(rng, extent, deviation, most, cuts=(), held_as=jnp.bfloat16):
    result = deviation * jax.random.normal(rng, extent, jnp.float32)
    if cuts:
        result = result * level_of(rng, extent, cuts, -0.22, 0.18)
    return jnp.clip(result, -most, most).astype(held_as)


def setup_inputs(seed: int = 0) -> dict:
    keys = jax.random.split(jax.random.key(seed), 9)
    return {
        "nodal_loads": centred(keys[0], (N_SEG, N_SUB, K, NI), 1.0, 6.0, ((0, 4), (1, 8)), jnp.float32),
        "schur_matrix": draw_schur_matrix(jax.random.fold_in(keys[8], 71), 0),
        "face_rows": jax.vmap(lambda own: jax.random.permutation(own, NI))(jax.random.split(keys[2], N_SEG * N_SUB)).reshape((N_SEG, N_SUB, NI)).astype(jnp.int32),
        "face_len": draw_face_len(jax.random.fold_in(keys[8], 71), 0),
        "relax_step": jnp.clip(jnp.exp(math.log(0.1) - 1.2039728 * jax.random.uniform(keys[4], (N_SEG, N_SUB), jnp.float32) ** level_of(keys[4], (N_SEG, N_SUB), ((0, 4), (1, 8)), -0.2, 0.2)), 0.03, 0.1),
        "coarse_basis": centred(keys[5], (N_SEG, N_SUB, 4, NI), (NI // 36) ** -0.5, 0.625, ((0, 4), (1, 8)), jnp.float32),
        "primal_index": draw_primal_index(jax.random.fold_in(keys[8], 71), 0),
        "coarse_inverse": draw_coarse_inverse(jax.random.fold_in(keys[8], 71), 0),
    }


HIGH = lax.Precision.HIGHEST

def symmetric(matrix):
    return 0.5 * (matrix + matrix.T)

def split_product(values, matrix):
    upper = values.astype(jnp.bfloat16)
    upper_back = lax.optimization_barrier(upper).astype(jnp.float32)
    lower = (values - upper_back).astype(jnp.bfloat16)
    first = jnp.dot(upper.astype(jnp.float32), matrix.astype(jnp.float32), preferred_element_type=jnp.float32)
    second = jnp.dot(lower.astype(jnp.float32), matrix.astype(jnp.float32), preferred_element_type=jnp.float32)
    return first + second

def reference(nodal_loads, schur_matrix, face_rows, face_len, relax_step, coarse_basis, primal_index, coarse_inverse):
    count = N_SEG * N_SUB
    flat_rows = face_rows.reshape(count, NI).astype(jnp.int32)
    face_len = face_len.astype(jnp.int32)
    zero_row = jnp.zeros((1, N_SUB), jnp.int32)
    lengths = jnp.stack([jnp.roll(face_len[:, :, 0], 1, axis=1), face_len[:, :, 0], jnp.concatenate([zero_row, face_len[:-1, :, 1]], axis=0), jnp.concatenate([face_len[:-1, :, 1], zero_row], axis=0)], axis=2).astype(jnp.int32)
    live_mask = (jnp.arange(NF, dtype=jnp.int32)[None, None, None, :] < lengths[..., None]).astype(jnp.float32)
    batch_ids = jnp.arange(count, dtype=jnp.int32)[:, None]
    weight_flat = jnp.zeros((count, NI), jnp.float32).at[batch_ids, flat_rows].set(jnp.float32(1.0) - jnp.float32(0.5) * live_mask.reshape(count, NI))
    inverse_rows = jnp.zeros((count, NI), jnp.int32).at[batch_ids, flat_rows].set(jnp.broadcast_to(jnp.arange(NI, dtype=jnp.int32)[None, :], (count, NI)))
    live_weight = weight_flat.reshape(N_SEG, N_SUB, 1, NI)
    schur_flat = schur_matrix.reshape(count, NI, NI)
    step_full = relax_step[:, :, None, None]
    face_ids = primal_index.reshape(count, 4).astype(jnp.int32)

    def assemble(values):
        flat = values.reshape(count, K, NI)
        slots = jnp.take_along_axis(flat, flat_rows[:, None, :], axis=2)
        slots = slots.reshape(N_SEG, N_SUB, K, 4, NF) * live_mask[:, :, None]
        zeros_plane = jnp.zeros_like(slots[:1, :, :, 0])
        left_in = jnp.roll(slots[:, :, :, 1], 1, axis=1)
        right_in = jnp.roll(slots[:, :, :, 0], -1, axis=1)
        down_in = jnp.concatenate([zeros_plane, slots[:-1, :, :, 3]], axis=0)
        up_in = jnp.concatenate([slots[1:, :, :, 2], zeros_plane], axis=0)
        received = jnp.stack([left_in, right_in, down_in, up_in], axis=3) * live_mask[:, :, None]
        received = received.reshape(count, K, NI)
        back = jnp.take_along_axis(received, inverse_rows[:, None, :], axis=2)
        return (flat + back).reshape(values.shape)

    def local_product(values):
        flat = values.reshape(count, K, NI)
        out = lax.map(lambda pair: split_product(pair[0], pair[1]), (flat, schur_flat))
        return out.reshape(values.shape)

    def inner(left, right):
        return jnp.einsum('abkn,abln->kl', left * live_weight, right, precision=HIGH)

    def precondition(resid):
        weighted = resid * live_weight
        solve = step_full * weighted
        for sweep in range(DEG):
            solve = step_full * weighted + solve - step_full * local_product(solve)
        local_coarse = jnp.einsum('abkn,abcn->abkc', weighted, coarse_basis, precision=HIGH)
        spread = jnp.transpose(local_coarse.reshape(count, K, 4), (1, 0, 2)).reshape(K, count * 4)
        coarse_sum = jnp.zeros((K, NP), jnp.float32).at[:, face_ids.reshape(-1)].add(spread)
        coarse_solution = jnp.dot(coarse_sum, coarse_inverse, precision=HIGH)
        picked = jnp.take(coarse_solution, face_ids, axis=1)
        picked = jnp.transpose(picked, (1, 0, 2)).reshape(N_SEG, N_SUB, K, 4)
        correction = jnp.einsum('abkc,abcn->abkn', picked, coarse_basis, precision=HIGH)
        return assemble((solve + correction) * live_weight)
    solution = jnp.zeros_like(nodal_loads)
    residual = assemble(nodal_loads)
    precond = precondition(residual)
    direction = precond
    rho = symmetric(inner(precond, residual))
    for iteration in range(ITERS):
        image = assemble(local_product(direction))
        curvature = symmetric(inner(direction, image))
        factor = jnp.linalg.cholesky(curvature)
        alpha = jax.scipy.linalg.cho_solve((factor, True), rho)
        solution = solution + jnp.einsum('kl,abkn->abln', alpha, direction, precision=HIGH)
        residual = residual - jnp.einsum('kl,abkn->abln', alpha, image, precision=HIGH)
        if iteration + 1 < ITERS:
            precond = precondition(residual)
            rho_next = symmetric(inner(precond, residual))
            factor_rho = jnp.linalg.cholesky(rho)
            beta = jax.scipy.linalg.cho_solve((factor_rho, True), rho_next)
            direction = precond + jnp.einsum('kl,abkn->abln', beta, direction, precision=HIGH)
            rho = rho_next
    return (solution, residual)
```

```python
import functools

import jax
import jax.numpy as jnp
from jax import lax
from jax.experimental import pallas as pl
from jax.experimental.pallas import tpu as pltpu
from jax.sharding import PartitionSpec as P

DEG = 3
ITERS = 3


HIGH = lax.Precision.HIGHEST


MESH = pl.DeviceIdType.MESH
LANES = 128


def greet(peers):
    barrier = pltpu.get_barrier_semaphore()
    for peer in peers:
        pl.semaphore_signal(barrier, inc=1, device_id=peer, device_id_type=MESH)
    pl.semaphore_wait(barrier, len(peers))


def total_kernel(counts, x_ref, o_ref, first, second, first_sems, second_sems):
    stages = (("sub", first, first_sems), ("seg", second, second_sems))
    places = {axis: lax.axis_index(axis) for axis in counts}

    def peer(axis, shift):
        return lax.rem(places[axis] + (shift + counts[axis]) % counts[axis], counts[axis])

    greet([{axis: peer(axis, d)} for axis, _, _ in stages for d in range(1, counts[axis])])
    value = x_ref[...]
    for stage, (axis, held, sems) in enumerate(stages):
        own = held.at[places[axis]]
        source = x_ref if stage == 0 else own
        held[places[axis]] = value
        sends = []
        for d in range(1, counts[axis]):
            send = pltpu.make_async_remote_copy(
                src_ref=source,
                dst_ref=own,
                send_sem=sems.at[0, d],
                recv_sem=sems.at[1, d],
                device_id={axis: peer(axis, d)},
                device_id_type=MESH,
            )
            send.start()
            sends.append(send)
        for d in range(1, counts[axis]):
            pltpu.make_async_remote_copy(
                src_ref=source,
                dst_ref=held.at[peer(axis, -d)],
                send_sem=sems.at[0, d],
                recv_sem=sems.at[1, d],
                device_id={axis: peer(axis, d)},
                device_id_type=MESH,
            ).wait_recv()
        for send in sends:
            send.wait_send()
        value = held[0]
        for i in range(1, counts[axis]):
            value = value + held[i]
    o_ref[...] = value


def global_sum(terms, collective_id):
    rows, columns = terms.shape
    padded = -(-columns // LANES) * LANES
    counts = {"sub": lax.axis_size("sub"), "seg": lax.axis_size("seg")}
    shape = (rows, padded)
    summed = pl.pallas_call(
        functools.partial(total_kernel, counts),
        out_shape=jax.ShapeDtypeStruct(shape, jnp.float32),
        in_specs=[pl.BlockSpec(memory_space=pltpu.VMEM)],
        out_specs=pl.BlockSpec(memory_space=pltpu.VMEM),
        scratch_shapes=[
            pltpu.VMEM((counts["sub"],) + shape, jnp.float32),
            pltpu.VMEM((counts["seg"],) + shape, jnp.float32),
            pltpu.SemaphoreType.DMA((2, counts["sub"])),
            pltpu.SemaphoreType.DMA((2, counts["seg"])),
        ],
        compiler_params=pltpu.CompilerParams(
            collective_id=collective_id, has_side_effects=True
        ),
    )(jnp.pad(terms, ((0, 0), (0, padded - columns))))
    return summed[:, :columns]


def halo_kernel(counts, slots_ref, mask_ref, o_ref, held, sems):
    width = slots_ref.shape[1] // 4

    def peer(axis, shift):
        count = counts[axis]
        return {axis: lax.rem(lax.axis_index(axis) + (shift + count) % count, count)}

    routes = (
        (1, 0, peer("sub", 1)),
        (0, 1, peer("sub", -1)),
        (3, 2, peer("seg", 1)),
        (2, 3, peer("seg", -1)),
    )
    greet([target for _, _, target in routes])
    copies = []
    for face, landing, target in routes:
        copy = pltpu.make_async_remote_copy(
            src_ref=slots_ref.at[:, pl.ds(face * width, width)],
            dst_ref=held.at[:, pl.ds(landing * width, width)],
            send_sem=sems.at[0, landing],
            recv_sem=sems.at[1, landing],
            device_id=target,
            device_id_type=MESH,
        )
        copy.start()
        copies.append(copy)
    for copy in copies:
        copy.wait()
    o_ref[...] = held[...] * mask_ref[...]


def exchange(slots, mask):
    counts = {"sub": lax.axis_size("sub"), "seg": lax.axis_size("seg")}
    return pl.pallas_call(
        functools.partial(halo_kernel, counts),
        out_shape=jax.ShapeDtypeStruct(slots.shape, jnp.float32),
        in_specs=[pl.BlockSpec(memory_space=pltpu.VMEM)] * 2,
        out_specs=pl.BlockSpec(memory_space=pltpu.VMEM),
        scratch_shapes=[
            pltpu.VMEM(slots.shape, jnp.float32),
            pltpu.SemaphoreType.DMA((2, 4)),
        ],
        compiler_params=pltpu.CompilerParams(collective_id=2, has_side_effects=True),
    )(slots, mask)


def symmetric(matrix):
    return 0.5 * (matrix + matrix.T)


def body(
    nodal_loads,
    schur_matrix,
    face_rows,
    face_len,
    relax_step,
    coarse_basis,
    primal_index,
    coarse_inverse,
):
    seg_at = lax.axis_index("seg")
    sub_at = lax.axis_index("sub")
    seg_count = lax.axis_size("seg")
    sub_count = lax.axis_size("sub")
    loads = nodal_loads[0, 0]
    matrix = schur_matrix[0, 0]
    slot_rows = face_rows[0, 0]
    relax = relax_step[0, 0]
    basis = coarse_basis[0, 0]
    width = matrix.shape[0]
    face_width = width // 4
    block = loads.shape[0]
    coarse_count = coarse_inverse.shape[0]
    lengths = jnp.stack(
        [
            face_len[seg_at, (sub_at + sub_count - 1) % sub_count, 0],
            face_len[seg_at, sub_at, 0],
            jnp.where(seg_at > 0, face_len[jnp.maximum(seg_at - 1, 0), sub_at, 1], 0),
            jnp.where(seg_at < seg_count - 1, face_len[seg_at, sub_at, 1], 0),
        ]
    )
    live_mask = (jnp.arange(face_width, dtype=jnp.int32)[None, :] < lengths[:, None]).astype(
        jnp.float32
    )
    mask_row = live_mask.reshape(1, width)
    placing = lax.optimization_barrier(
        (slot_rows[:, None] == jnp.arange(width, dtype=jnp.int32)[None, :]).astype(jnp.bfloat16)
    )
    covered = jnp.dot(
        jnp.broadcast_to(mask_row.astype(jnp.bfloat16), (16, width)),
        placing,
        preferred_element_type=jnp.float32,
    )
    live_weight = 1.0 - 0.5 * covered[0]
    my_faces = primal_index[seg_at, sub_at]
    coarse_columns = jnp.take(coarse_inverse, my_faces, axis=1)

    def split_dot(values, right, contract):
        upper = values.astype(jnp.bfloat16)
        upper_back = lax.optimization_barrier(upper).astype(jnp.float32)
        lower = (values - upper_back).astype(jnp.bfloat16)
        stacked = jnp.concatenate([upper, lower], axis=0)
        both = lax.dot_general(
            stacked,
            right,
            (((1,), (contract,)), ((), ())),
            preferred_element_type=jnp.float32,
        )
        return both[:block] + both[block:]

    def assemble(values):
        slots = split_dot(values, placing, 1)
        return values + split_dot(exchange(slots, mask_row), placing, 0)

    def local_product(values):
        return split_dot(values, matrix, 0)

    def global_inner(local_terms):
        return global_sum(local_terms, 0)

    def precondition(weighted):
        solve = relax * weighted
        for sweep in range(DEG):
            solve = relax * weighted + solve - relax * local_product(solve)
        local_coarse = jnp.dot(weighted, basis.T, precision=HIGH)
        table = (my_faces[:, None] == jnp.arange(coarse_count, dtype=jnp.int32)[None, :]).astype(
            jnp.float32
        )
        coarse_sum = global_sum(jnp.dot(local_coarse, table, precision=HIGH), 1)
        picked = jnp.dot(coarse_sum, coarse_columns, precision=HIGH)
        correction = jnp.dot(picked, basis, precision=HIGH)
        return assemble((solve + correction) * live_weight[None, :])

    solution = jnp.zeros_like(loads)
    partial_residual = loads
    assembled = assemble(partial_residual)
    precond = precondition(assembled * live_weight[None, :])
    direction = precond
    rho = symmetric(global_inner(jnp.dot(precond, partial_residual.T, precision=HIGH)))
    for iteration in range(ITERS):
        partial_image = local_product(direction)
        curvature = symmetric(global_inner(jnp.dot(direction, partial_image.T, precision=HIGH)))
        factor = jnp.linalg.cholesky(curvature)
        alpha = jax.scipy.linalg.cho_solve((factor, True), rho)
        solution = solution + jnp.dot(alpha.T, direction, precision=HIGH)
        partial_residual = partial_residual - jnp.dot(alpha.T, partial_image, precision=HIGH)
        assembled = assemble(partial_residual)
        if iteration + 1 < ITERS:
            precond = precondition(assembled * live_weight[None, :])
            rho_next = symmetric(global_inner(jnp.dot(precond, partial_residual.T, precision=HIGH)))
            factor_rho = jnp.linalg.cholesky(rho)
            beta = jax.scipy.linalg.cho_solve((factor_rho, True), rho_next)
            direction = precond + jnp.dot(beta.T, direction, precision=HIGH)
            rho = rho_next
    return (solution[None, None], assembled[None, None])


def solution(mesh):
    placed = (
        P("seg", "sub", None, None),
        P("seg", "sub", None, None),
        P("seg", "sub", None),
        P(),
        P("seg", "sub"),
        P("seg", "sub", None, None),
        P(),
        P(),
    )
    return jax.shard_map(
        body,
        mesh=mesh,
        in_specs=placed,
        out_specs=(P("seg", "sub", None, None), P("seg", "sub", None, None)),
        check_vma=False,
    )
```
